512 devices in a mesh: blk: 64 (over z_lo, x, core), group: 8 (over z_hi, y).
Axes of the slice: x: 4, y: 4, z: 16 (z_hi: 2, z_lo: 8; z = z_hi * 8 + z_lo), core: 2. Of those that a mesh axis runs over, the one named last changes fastest.
Arguments:
- user_factors: float32 [8, 65536, 256], P('group', 'blk'), may hold values from -1.5 to 1.5
- item_factors: float32 [8, 16384, 256], P('group', 'blk'), may hold values from -1.5 to 1.5
- ratings: bfloat16 [8, 64, 8, 2, 256, 256], P('group', 'blk'), may hold values from -6 to 6
- tile_rows: int32 [8, 64, 8, 2], P('group', 'blk'), may hold values from 0 to 3, as said below
- counts: int32 [8, 64, 8], P('group', 'blk'), may hold values from 0 to 2
- plan: int32 [8, 64], replicated, may hold values from 0 to 63, as said below
Outputs:
- user_out: float32 [8, 65536, 256], P('group', 'blk')
- received: bfloat16 [8, 64, 4, 256, 256], P('group', 'blk')
The draws below stay inside these ranges and needn't reach their ends.
Inputs may be any that keep to these rules, and one draw needn't show every extreme that they name: `tile_rows`: within one stop of one device the 2 entries differ. `plan`: in every group no device receives more than 4 blocks, and some device receives exactly 4.
All inputs are finite; a program needn't handle non-finite values.
Results may differ from the reference program's by a relative error of at most 0.006.
Values may be sent and summed in bfloat16 or wider, within the bound.
No kernel may reach another device: no remote copies, remote signals or barrier semaphores. Data moves between devices by JAX's collectives and lax.ppermute only.
A program may use at most 64 MiB of HBM per device.

```python
import jax
import jax.numpy as jnp
from jax import lax

R = 256
TILE = 256
UB = 1024
CAPT = 2
CAP = 4
IB = 256
BLOCKS = 64
GROUPS = 8
STOPS = 8
USERS = 65536
ITEMS = 16384


def factor_draw(key, rows):
    return 0.25 * jax.random.truncated_normal(key, -6.0, 6.0, (GROUPS, rows, R), jnp.float32)


def draw_user_factors(key, part):
    return factor_draw(jax.random.fold_in(key, 11), USERS)


def draw_item_factors(key, part):
    return factor_draw(jax.random.fold_in(key, 23), ITEMS)


def draw_tile_rows(key, part):
    rows_per = UB // TILE
    scores = jax.random.randint(key, (GROUPS, BLOCKS, STOPS, rows_per), 0, 1 << 20) * rows_per + jnp.arange(rows_per)
    ranked = jnp.argsort(scores, axis=-1, stable=True).astype(jnp.int32)
    return ranked[..., :CAPT]


def draw_plan(key, part):

    def one_group(group_id):
        group_key = jax.random.fold_in(key, group_id)
        first_key, second_key = jax.random.split(group_key)
        block_order = jax.random.permutation(first_key, BLOCKS)
        devices = jax.random.permutation(second_key, BLOCKS)
        positions = jnp.arange(BLOCKS)
        device_slot = jnp.where(positions < CAP, 0, 1 + (positions - CAP) // 2)
        targets = devices[device_slot]
        return jnp.zeros((BLOCKS,), jnp.int32).at[block_order].set(targets.astype(jnp.int32))
    return jax.vmap(one_group)(jnp.arange(GROUPS)).astype(jnp.int32)


def place_ends(values, stream_key, least, high):
    place = [jax.random.randint(jax.random.fold_in(stream_key, axis), (), 0, length) for axis, length in enumerate(values.shape)]
    main_axis = values.shape.index(max(values.shape))
    neighbour = place[:main_axis] + [(place[main_axis] + 1) % values.shape[main_axis]] + place[main_axis + 1:]
    return values.at[tuple(place)].set(least).at[tuple(neighbour)].set(high)


def block_levels(stream_key, extent, pieces, smallest, largest):
    def one(dim, parts):
        draws = jax.random.uniform(jax.random.fold_in(jax.random.fold_in(stream_key, 6), dim), (parts,), jnp.float32, smallest / len(pieces), largest / len(pieces))
        return jnp.repeat(jnp.exp(draws), extent[dim] // parts).reshape((-1,) + (1,) * (len(extent) - dim - 1))

    loudness = one(*pieces[0])
    for cut in pieces[1:]:
        loudness = loudness * one(*cut)
    return loudness


def scatter_about(key, shape, width, most, pieces=(), dtype=jnp.bfloat16):
    values = jax.random.normal(key, shape, jnp.float32) * width
    if len(pieces) > 0:
        values = block_levels(key, shape, pieces, -0.22, 0.18) * values
    return jnp.clip(values, min=-most, max=most).astype(dtype)


def setup_inputs(seed: int = 0) -> dict:
    seeds = jax.random.split(jax.random.key(seed), 7)
    user_factors = draw_user_factors(jax.random.fold_in(seeds[6], 71), 0)
    item_factors = draw_item_factors(jax.random.fold_in(seeds[6], 71), 0)
    ratings = scatter_about(seeds[2], (GROUPS, BLOCKS, STOPS, CAPT, TILE, TILE), 1.0, 6.0, ((0, 8), (1, 64)))
    tile_rows = draw_tile_rows(jax.random.fold_in(seeds[6], 71), 0)
    counts = place_ends(jax.random.randint(seeds[4], (GROUPS, BLOCKS, STOPS), 0, CAPT + 1), jax.random.fold_in(seeds[4], 1), 0, CAPT).astype(jnp.int32)
    plan = draw_plan(jax.random.fold_in(seeds[6], 71), 0)
    return {"user_factors": user_factors, "item_factors": item_factors, "ratings": ratings, "tile_rows": tile_rows, "counts": counts, "plan": plan}


learn_rate = 0.01
shrinkage = 0.05


def round_trip(values):
    return lax.optimization_barrier(values.astype(jnp.bfloat16)).astype(jnp.float32)


def reference(user_factors, item_factors, ratings, tile_rows, counts, plan):
    rows_per = UB // TILE
    user_rows = user_factors.reshape(GROUPS, BLOCKS, rows_per, TILE, R)
    item_block = item_factors.reshape(GROUPS, BLOCKS, IB, R)
    slot_ids = jnp.arange(CAPT)
    for stop_index in range(STOPS):
        if stop_index > 0:
            item_block = jnp.roll(item_block, 1, axis=1)
        selector = (tile_rows[:, :, stop_index, :, None] == jnp.arange(rows_per)[None, None, None, :]).astype(jnp.float32)
        before = jnp.einsum("gbcr,gbrtk->gbctk", selector, user_rows, precision=lax.Precision.HIGHEST)
        active = (slot_ids[None, None, :] < counts[:, :, stop_index, None]).astype(jnp.float32)
        user_low = round_trip(before)
        item_low = round_trip(item_block)
        predicted = jnp.einsum("gbctk,gbik->gbcti", user_low, item_low)
        residual = round_trip(active[..., None, None] * (ratings[:, :, stop_index].astype(jnp.float32) - predicted))
        change = learn_rate * active[..., None, None] * (jnp.einsum("gbcti,gbik->gbctk", residual, item_low) - shrinkage * before)
        user_rows = user_rows + jnp.einsum("gbcr,gbctk->gbrtk", selector, change, precision=lax.Precision.HIGHEST)
        grad_items = jnp.einsum("gbcti,gbctk->gbik", residual, user_low)
        tile_count = counts[:, :, stop_index, None, None].astype(jnp.float32)
        item_block = item_block + learn_rate * (grad_items - shrinkage * tile_count * item_block)
    at_home = jnp.roll(item_block, -(STOPS - 1), axis=1)
    handed = round_trip(at_home)
    positions = jnp.arange(BLOCKS)
    same_dest = plan[:, :, None] == plan[:, None, :]
    earlier = positions[None, None, :] < positions[None, :, None]
    slot_of = jnp.sum((same_dest & earlier).astype(jnp.int32), axis=2)
    selector = ((plan[:, None, None, :] == positions[None, :, None, None]) & (slot_of[:, None, None, :] == jnp.arange(CAP)[None, None, :, None])).astype(jnp.float32)
    shifted = jnp.einsum("gdck,gkir->gdcir", selector, handed, precision=lax.Precision.HIGHEST).astype(jnp.bfloat16)
    received = jnp.roll(shifted, 1, axis=0)
    return user_rows.reshape(GROUPS, USERS, R), received
```

```python
import functools

import jax
import jax.numpy as jnp
from jax import lax
from jax.experimental import pallas as pl
from jax.experimental.pallas import tpu as pltpu
from jax.sharding import PartitionSpec as P

CAP = 4
PLANE = 8
LAG = 1


learn_rate = 0.01
shrinkage = 0.05

VMEM = pl.BlockSpec(memory_space=pltpu.VMEM)
SMEM = pl.BlockSpec(memory_space=pltpu.SMEM)
ANY = pl.BlockSpec(memory_space=pl.ANY)
F32 = jnp.float32
BF16 = jnp.bfloat16


def call(body, name, out_shape, in_specs, out_specs, scratch=(), flops=0, moved=1 << 20, alias={}):
    return pl.pallas_call(
        body,
        name=name,
        out_shape=out_shape,
        in_specs=in_specs,
        out_specs=out_specs,
        scratch_shapes=scratch,
        input_output_aliases=alias,
        cost_estimate=pl.CostEstimate(flops=flops, bytes_accessed=moved, transcendentals=0),
        compiler_params=pltpu.CompilerParams(vmem_limit_bytes=12 << 20),
    )


def plan_slot(slot, stops, count_ref):
    inner = lax.rem(lax.axis_index("blk"), PLANE)
    early = jnp.logical_and(slot <= inner, slot < stops)
    late = jnp.logical_and(slot > inner + LAG, slot < stops + LAG)
    active = jnp.logical_or(early, late)
    stop = jnp.clip(jnp.where(late, slot - LAG, slot), 0, stops - 1)
    count = jnp.where(active, count_ref[stop], 0)
    crossed = jnp.logical_and(late, inner == 0)
    return active, stop, count, crossed


def fetch(stop, count, row_ref, ratings_ref, user_ref, low_ref, rated_ref, tiles, sem):
    tile = tiles.shape[1]
    for c in range(tiles.shape[0]):
        rows = pl.ds(c * tile, tile)

        @pl.when(c < count)
        def _():
            first = pl.multiple_of(row_ref[c, stop] * tile, tile)
            low_ref[rows, :] = user_ref[pl.ds(first, tile), :].astype(BF16)

        @pl.when(c >= count)
        def _():
            low_ref[rows, :] = jnp.zeros((tile, low_ref.shape[1]), BF16)
            rated_ref[:, rows] = jnp.zeros((rated_ref.shape[0], tile), BF16)

    pltpu.make_async_copy(ratings_ref.at[stop], tiles, sem).wait()
    for c in range(tiles.shape[0]):
        rows = pl.ds(c * tile, tile)

        @pl.when(c < count)
        def _():
            rated_ref[:, rows] = tiles[c].T


def first_body(stops, count_ref, row_ref, user_ref, ratings_ref, out_ref, low_ref, rated_ref, tiles, sem):
    pltpu.make_async_copy(ratings_ref.at[0], tiles, sem).start()
    out_ref[...] = user_ref[...]
    fetch(0, count_ref[0], row_ref, ratings_ref, user_ref, low_ref, rated_ref, tiles, sem)


def item_body(slot, stops, last, n_in, count_ref, *refs):
    sources = refs[:n_in]
    low_ref, rated_ref, next_ref, residual_ref, item_ref, block = refs[n_in:]
    active, _, count, crossed = plan_slot(slot, stops, count_ref)
    if slot == 0:
        exact = sources[0][...]
        item_low = exact.astype(BF16)
    else:
        @pl.when(jnp.logical_not(active))
        def _():
            block[...] = sources[1][...]

        if n_in == 2:
            @pl.when(active)
            def _():
                block[...] = sources[0][...]
        else:
            @pl.when(jnp.logical_and(active, jnp.logical_not(crossed)))
            def _():
                block[...] = sources[0][...]

            @pl.when(crossed)
            def _():
                block[...] = sources[2][...]

        item_low = block[...]
        exact = item_low.astype(F32)
    item_ref[...] = item_low
    low = low_ref[...]
    predicted = lax.dot_general(
        item_low, low, (((1,), (1,)), ((), ())), preferred_element_type=F32
    )
    residual = (rated_ref[...].astype(F32) - predicted).astype(BF16)
    residual_ref[...] = residual
    grad = jnp.dot(residual, low, preferred_element_type=F32)
    decay = shrinkage * count.astype(F32)
    updated = (exact + learn_rate * (grad - decay * exact)).astype(BF16)
    if last:
        groups, halves, rows, columns = next_ref.shape
        for h in range(halves):
            half = updated[:, h * columns : (h + 1) * columns]
            next_ref[:, h] = half.reshape(groups, rows, columns)
    else:
        next_ref[...] = updated


def user_body(slot, stops, last, count_ref, row_ref, residual_ref, item_ref, user_ref, *refs):
    _, stop, count, _ = plan_slot(slot, stops, count_ref)
    if last:
        (out_ref,) = refs
    else:
        ratings_ref, out_ref, low_ref, rated_ref, tiles, sem = refs
        _, next_stop, next_count, _ = plan_slot(slot + 1, stops, count_ref)
        pltpu.make_async_copy(ratings_ref.at[next_stop], tiles, sem).start()
    tile = item_ref.shape[0]
    out_ref[...] = user_ref[...]
    for c in range(residual_ref.shape[1] // tile):

        @pl.when(c < count)
        def _():
            step = lax.dot_general(
                residual_ref[:, c * tile : (c + 1) * tile],
                item_ref[...],
                (((0,), (0,)), ((), ())),
                preferred_element_type=F32,
            )
            rows = pl.ds(pl.multiple_of(row_ref[c, stop] * tile, tile), tile)
            before = user_ref[rows, :]
            out_ref[rows, :] = before + learn_rate * (step - shrinkage * before)

    if not last:
        fetch(next_stop, next_count, row_ref, ratings_ref, out_ref, low_ref, rated_ref, tiles, sem)


def route_body(stops, plan_ref, index_ref, filled):
    groups, blocks = plan_ref.shape
    group = lax.rem(lax.axis_index("group") + groups - 1, groups)

    @pl.loop(0, blocks)
    def _(d):
        filled[d] = 0
        for c in range(CAP):
            index_ref[d * CAP + c] = -1

    @pl.loop(0, blocks)
    def _(k):
        dest = plan_ref[group, k]
        place = filled[dest]
        filled[dest] = place + 1
        index_ref[dest * CAP + place] = lax.rem(k + (stops - 1), blocks)


def pick_body(index_ref, pieces_ref, out_ref):
    @pl.loop(0, out_ref.shape[0])
    def _(d):
        for c in range(CAP):
            at = index_ref[d * CAP + c]
            piece = pieces_ref[jnp.maximum(at, 0)]
            out_ref[d, c] = jnp.where(at >= 0, piece, jnp.zeros_like(piece))


def place_body(pieces_ref, out_ref):
    groups, halves, slots, rows, columns = pieces_ref.shape
    for c in range(slots):
        for h in range(halves):
            out_ref[c, :, h * columns : (h + 1) * columns] = pieces_ref[:, h, c].reshape(
                groups * rows, columns
            )


def shards(user_factors, item_factors, ratings, tile_rows, counts, plan):
    users = user_factors[0]
    rating_tiles = ratings[0, 0]
    row_table = tile_rows[0, 0].T
    count_table = counts[0, 0]
    stops, tiles_at_stop, tile, _ = rating_tiles.shape
    blocks = lax.axis_size("blk")
    groups = lax.axis_size("group")
    items, rank = item_factors.shape[1:]
    wide = tiles_at_stop * tile
    slots = stops + LAG

    index = call(
        functools.partial(route_body, stops),
        "route",
        jax.ShapeDtypeStruct((blocks * CAP,), jnp.int32),
        [SMEM],
        SMEM,
        [pltpu.SMEM((blocks,), jnp.int32)],
        moved=4 * blocks,
    )(plan)

    low_shape = jax.ShapeDtypeStruct((wide, rank), BF16)
    rated_shape = jax.ShapeDtypeStruct((items, wide), BF16)
    block_shape = jax.ShapeDtypeStruct((items, rank), BF16)
    piece_shape = jax.ShapeDtypeStruct((items // 8, rank // 128, 8, 128), BF16)
    user_shape = jax.ShapeDtypeStruct(users.shape, F32)
    tile_scratch = [pltpu.VMEM((tiles_at_stop, tile, tile), BF16), pltpu.SemaphoreType.DMA]
    users, low, rated = call(
        functools.partial(first_body, stops),
        "first",
        (user_shape, low_shape, rated_shape),
        [SMEM, SMEM, VMEM, ANY],
        (VMEM, VMEM, VMEM),
        tile_scratch,
    )(count_table, row_table, users, rating_tiles)

    within = [(b, b + 1) for b in range(blocks) if b % PLANE != PLANE - 1]
    across = [(b, (b + 1) % blocks) for b in range(PLANE - 1, blocks, PLANE)]
    arrived = [item_factors[0]]
    crossing = {}
    for slot in range(slots):
        last = slot == slots - 1
        block, residual, item_low = call(
            functools.partial(item_body, slot, stops, last, len(arrived)),
            f"items_{slot}",
            (piece_shape if last else block_shape, rated_shape, block_shape),
            [SMEM] + [VMEM] * (len(arrived) + 2),
            (VMEM, VMEM, VMEM),
            [pltpu.VMEM((items, rank), BF16)],
            4 * items * wide * rank,
        )(count_table, *arrived, low, rated)
        if not last:
            arrived = [lax.ppermute(block, "blk", within), block]
            if slot < stops - 1:
                crossing[slot + 1 + LAG] = lax.ppermute(block, "blk", across)
            if slot + 1 in crossing:
                arrived.append(crossing[slot + 1])
        body = functools.partial(user_body, slot, stops, last)
        operands = (count_table, row_table, residual, item_low, users)
        flops = 2 * wide * items * rank
        if last:
            users = call(
                body, f"users_{slot}", user_shape, [SMEM, SMEM, VMEM, VMEM, VMEM], VMEM, (), flops
            )(*operands)
        else:
            users, low, rated = call(
                body,
                f"users_{slot}",
                (user_shape, low_shape, rated_shape),
                [SMEM, SMEM, VMEM, VMEM, VMEM, ANY],
                (VMEM, VMEM, VMEM),
                tile_scratch,
                flops,
                alias={4: 0},
            )(*operands, rating_tiles)

    pieces = block.reshape(blocks, -1, 128)
    shifted = lax.ppermute(pieces, "group", [(g, (g + 1) % groups) for g in range(groups)])
    spread = lax.all_to_all(shifted, "blk", split_axis=0, concat_axis=0, tiled=True)
    picked = call(
        pick_body,
        "pick",
        jax.ShapeDtypeStruct((blocks, CAP) + pieces.shape[1:], BF16),
        [SMEM, VMEM],
        VMEM,
    )(index, spread)
    landed = lax.all_to_all(picked, "blk", split_axis=0, concat_axis=0, tiled=True)
    landed = landed.reshape(blocks, CAP, -1, 8, 128).transpose(0, 2, 1, 3, 4)
    received = call(
        place_body, "place", jax.ShapeDtypeStruct((CAP, items, rank), BF16), [VMEM], VMEM
    )(landed.reshape(items // 8, rank // 128, CAP, 8, 128))
    return (users[None], received[None, None])


def solution(mesh):
    in_specs = (
        P("group", "blk", None),
        P("group", "blk", None),
        P("group", "blk", None, None, None, None),
        P("group", "blk", None, None),
        P("group", "blk", None),
        P(),
    )
    out_specs = (P("group", "blk", None), P("group", "blk", None, None, None))
    return jax.shard_map(shards, mesh=mesh, in_specs=in_specs, out_specs=out_specs, check_vma=False)
```

```python
import functools

import jax
import jax.numpy as jnp
from jax import lax
from jax.experimental import pallas as pl
from jax.experimental.pallas import tpu as pltpu
from jax.sharding import PartitionSpec as P


CAP = 4
PLANE = 8
LAG = 2


FIRST_LIMIT = 62_500_000

learn_rate = 0.01
shrinkage = 0.05

VMEM = pl.BlockSpec(memory_space=pltpu.VMEM)
SMEM = pl.BlockSpec(memory_space=pltpu.SMEM)
ANY = pl.BlockSpec(memory_space=pl.ANY)
HBM = pl.BlockSpec(memory_space=pltpu.MemorySpace.HBM)
F32 = jnp.float32
BF16 = jnp.bfloat16


def call(
    body, out_shape, in_specs, out_specs, scratch=(), flops=0, moved=1 << 20, alias={},
    limit=12 << 20,
):
    return pl.pallas_call(
        body,
        out_shape=out_shape,
        in_specs=in_specs,
        out_specs=out_specs,
        scratch_shapes=scratch,
        input_output_aliases=alias,
        cost_estimate=pl.CostEstimate(flops=flops, bytes_accessed=moved, transcendentals=0),
        compiler_params=pltpu.CompilerParams(vmem_limit_bytes=limit),
    )


def stop_at(slot, inner, stops):
    if slot <= inner and slot < stops:
        return slot
    return slot - LAG if inner + LAG < slot < stops + LAG else None


def plan_slot(slot, stops, count_ref):
    inner = lax.rem(lax.axis_index("blk"), PLANE)
    early = jnp.logical_and(slot <= inner, slot < stops)
    late = jnp.logical_and(slot > inner + LAG, slot < stops + LAG)
    active = jnp.logical_or(early, late)
    stop = jnp.clip(jnp.where(late, slot - LAG, slot), 0, stops - 1)
    count = jnp.where(active, count_ref[stop], 0)
    crossed = jnp.logical_and(late, inner == 0)
    return active, stop, count, crossed


def fetch(stop, count, row_ref, user_ref, low_ref, rated_ref, tiles, copy):
    tile = tiles.shape[1]
    for c in range(tiles.shape[0]):
        rows = pl.ds(c * tile, tile)

        @pl.when(c < count)
        def _():
            first = pl.multiple_of(row_ref[c, stop] * tile, tile)
            low_ref[rows, :] = user_ref[pl.ds(first, tile), :].astype(BF16)

        @pl.when(c >= count)
        def _():
            low_ref[rows, :] = jnp.zeros((tile, low_ref.shape[1]), BF16)
            rated_ref[:, rows] = jnp.zeros((rated_ref.shape[0], tile), BF16)

    copy.wait()
    for c in range(tiles.shape[0]):
        rows = pl.ds(c * tile, tile)

        @pl.when(c < count)
        def _():
            rated_ref[:, rows] = tiles[c].T


def update_items(exact, item_low, count, low_ref, rated_ref, residual_ref, item_ref):
    item_ref[...] = item_low
    tile = item_ref.shape[0]
    grad = None
    for c in range(low_ref.shape[0] // tile):
        span = slice(c * tile, (c + 1) * tile)
        low = low_ref[span, :]
        predicted = lax.dot_general(
            item_low, low, (((1,), (1,)), ((), ())), preferred_element_type=F32
        )
        residual = (rated_ref[:, span].astype(F32) - predicted).astype(BF16)
        residual_ref[:, span] = residual
        part = jnp.dot(residual, low, preferred_element_type=F32)
        grad = part if grad is None else grad + part
    decay = shrinkage * count.astype(F32)
    return (exact + learn_rate * (grad - decay * exact)).astype(BF16)


def first_body(
    count_hbm, row_hbm, user_hbm, item_hbm, ratings_hbm, next_ref, residual_ref, item_ref,
    count_ref, row_ref, user_ref, exact_ref, tiles, low_ref, rated_ref, sems,
):
    pairs = [
        (count_hbm, count_ref),
        (row_hbm, row_ref),
        (user_hbm, user_ref),
        (item_hbm, exact_ref),
        (ratings_hbm.at[0], tiles),
    ]
    moves = [pltpu.make_async_copy(*pair, sems.at[n]) for n, pair in enumerate(pairs)]
    for move in moves:
        move.start()
    for move in moves[:3]:
        move.wait()
    count = count_ref[0]
    fetch(0, count, row_ref, user_ref, low_ref, rated_ref, tiles, moves[4])
    moves[3].wait()
    exact = exact_ref[...]
    next_ref[...] = update_items(
        exact, exact.astype(BF16), count, low_ref, rated_ref, residual_ref, item_ref
    )


def item_body(slot, stops, last, n_in, count_ref, *refs):
    sources = refs[:n_in]
    low_ref, rated_ref, next_ref, residual_ref, item_ref = refs[n_in:]
    active, _, count, crossed = plan_slot(slot, stops, count_ref)

    def emit(block):
        if last:
            groups, halves, rows, columns = next_ref.shape
            for h in range(halves):
                half = block[:, h * columns : (h + 1) * columns]
                next_ref[:, h] = half.reshape(groups, rows, columns)
        else:
            next_ref[...] = block

    @pl.when(active)
    def _():
        item_low = sources[0][...]
        if n_in == 3:
            item_low = jnp.where(crossed, sources[2][...], item_low)
        exact = item_low.astype(F32)
        emit(update_items(exact, item_low, count, low_ref, rated_ref, residual_ref, item_ref))

    @pl.when(jnp.logical_not(active))
    def _():
        emit(sources[1][...])


def user_body(slot, stops, last, count_ref, row_ref, residual_ref, item_ref, user_ref, *refs):
    _, stop, count, _ = plan_slot(slot, stops, count_ref)
    if last:
        (out_ref,) = refs
    else:
        ratings_ref, out_ref, low_ref, rated_ref, tiles, sem = refs
        next_active, next_stop, next_count, _ = plan_slot(slot + 1, stops, count_ref)
        copy = pltpu.make_async_copy(ratings_ref.at[next_stop], tiles, sem)
        pl.when(next_active)(copy.start)
    tile = item_ref.shape[0]
    out_ref[...] = user_ref[...]
    for c in range(residual_ref.shape[1] // tile):

        @pl.when(c < count)
        def _():
            step = lax.dot_general(
                residual_ref[:, c * tile : (c + 1) * tile],
                item_ref[...],
                (((0,), (0,)), ((), ())),
                preferred_element_type=F32,
            )
            rows = pl.ds(pl.multiple_of(row_ref[c, stop] * tile, tile), tile)
            before = user_ref[rows, :]
            out_ref[rows, :] = before + learn_rate * (step - shrinkage * before)

    if not last:

        @pl.when(next_active)
        def _():
            fetch(next_stop, next_count, row_ref, out_ref, low_ref, rated_ref, tiles, copy)


def route_body(stops, plan_ref, index_ref, filled):
    groups, blocks = plan_ref.shape
    group = lax.rem(lax.axis_index("group") + groups - 1, groups)

    @pl.loop(0, blocks)
    def _(d):
        filled[d] = 0
        for c in range(CAP):
            index_ref[d * CAP + c] = -1

    @pl.loop(0, blocks)
    def _(k):
        dest = plan_ref[group, k]
        place = filled[dest]
        filled[dest] = place + 1
        index_ref[dest * CAP + place] = lax.rem(k + (stops - 1), blocks)


def pick_body(index_ref, pieces_ref, out_ref):
    @pl.loop(0, out_ref.shape[0], unroll=8)
    def _(d):
        for c in range(CAP):
            at = index_ref[d * CAP + c]
            piece = pieces_ref[jnp.maximum(at, 0)]
            out_ref[d, c] = jnp.where(at >= 0, piece, jnp.zeros_like(piece))


def place_body(pieces_ref, out_ref):
    groups, halves, slots, rows, columns = pieces_ref.shape
    for c in range(slots):
        for h in range(halves):
            out_ref[c, :, h * columns : (h + 1) * columns] = pieces_ref[:, h, c].reshape(
                groups * rows, columns
            )


def shards(user_factors, item_factors, ratings, tile_rows, counts, plan):
    users = user_factors[0]
    rating_tiles = ratings[0, 0]
    row_table = tile_rows[0, 0].T
    count_table = counts[0, 0]
    stops, tiles_at_stop, tile, _ = rating_tiles.shape
    blocks = lax.axis_size("blk")
    groups = lax.axis_size("group")
    items, rank = item_factors.shape[1:]
    wide = tiles_at_stop * tile
    slots = stops + LAG

    index = call(
        functools.partial(route_body, stops),
        jax.ShapeDtypeStruct((blocks * CAP,), jnp.int32),
        [SMEM],
        SMEM,
        [pltpu.SMEM((blocks,), jnp.int32)],
        moved=4 * blocks,
    )(plan)

    low_shape = jax.ShapeDtypeStruct((wide, rank), BF16)
    rated_shape = jax.ShapeDtypeStruct((items, wide), BF16)
    block_shape = jax.ShapeDtypeStruct((items, rank), BF16)
    piece_shape = jax.ShapeDtypeStruct((items // 8, rank // 128, 8, 128), BF16)
    user_shape = jax.ShapeDtypeStruct(users.shape, F32)
    tile_scratch = [pltpu.VMEM((tiles_at_stop, tile, tile), BF16), pltpu.SemaphoreType.DMA]
    block, residual, item_low = call(
        first_body,
        (block_shape, rated_shape, block_shape),
        [HBM] * 5,
        (VMEM, VMEM, VMEM),
        [
            pltpu.SMEM(count_table.shape, jnp.int32),
            pltpu.SMEM(row_table.shape, jnp.int32),
            pltpu.VMEM(users.shape, F32),
            pltpu.VMEM((items, rank), F32),
            tile_scratch[0],
            pltpu.VMEM(low_shape.shape, BF16),
            pltpu.VMEM(rated_shape.shape, BF16),
            pltpu.SemaphoreType.DMA((5,)),
        ],
        4 * items * wide * rank,
        limit=FIRST_LIMIT,
    )(count_table, row_table, users, item_factors[0], rating_tiles)

    across = [(b, (b + 1) % blocks) for b in range(PLANE - 1, blocks, PLANE)]
    crossing = {}
    for slot in range(slots):
        last = slot == slots - 1
        if slot > 0:
            block, residual, item_low = call(
                functools.partial(item_body, slot, stops, last, len(arrived)),
                (piece_shape if last else block_shape, rated_shape, block_shape),
                [SMEM] + [VMEM] * (len(arrived) + 2),
                (VMEM, VMEM, VMEM),
                (),
                4 * items * wide * rank,
            )(count_table, *arrived, low, rated)
        if not last:
            within = [
                (b, b + 1)
                for b in range(blocks)
                if b % PLANE != PLANE - 1
                and stop_at(slot, b % PLANE, stops) is not None
                and stop_at(slot + 1, b % PLANE + 1, stops) == stop_at(slot, b % PLANE, stops) + 1
            ]
            arrived = [lax.ppermute(block, "blk", within), block]
            if slot < stops - 1:
                crossing[slot + 1 + LAG] = lax.ppermute(block, "blk", across)
            if slot + 1 in crossing:
                arrived.append(crossing[slot + 1])
        body = functools.partial(user_body, slot, stops, last)
        operands = (count_table, row_table, residual, item_low, users)
        flops = 2 * wide * items * rank
        if last:
            users = call(
                body, user_shape, [SMEM, SMEM, VMEM, VMEM, VMEM], VMEM, (), flops
            )(*operands)
        else:
            users, low, rated = call(
                body,
                (user_shape, low_shape, rated_shape),
                [SMEM, SMEM, VMEM, VMEM, VMEM, ANY],
                (VMEM, VMEM, VMEM),
                tile_scratch,
                flops,
                alias={4: 0} if slot else {},
            )(*operands, rating_tiles)

    pieces = block.reshape(blocks, -1, 128)
    shifted = lax.ppermute(pieces, "group", [(g, (g + 1) % groups) for g in range(groups)])
    spread = lax.all_to_all(shifted, "blk", split_axis=0, concat_axis=0, tiled=True)
    picked = call(
        pick_body, jax.ShapeDtypeStruct((blocks, CAP) + pieces.shape[1:], BF16), [SMEM, VMEM], VMEM
    )(index, spread)
    landed = lax.all_to_all(picked, "blk", split_axis=0, concat_axis=0, tiled=True)
    landed = landed.reshape(blocks, CAP, -1, 8, 128).transpose(0, 2, 1, 3, 4)
    received = call(
        place_body, jax.ShapeDtypeStruct((CAP, items, rank), BF16), [VMEM], VMEM
    )(landed.reshape(items // 8, rank // 128, CAP, 8, 128))
    return (users[None], received[None, None])


def solution(mesh):
    in_specs = (
        P("group", "blk", None),
        P("group", "blk", None),
        P("group", "blk", None, None, None, None),
        P("group", "blk", None, None),
        P("group", "blk", None),
        P(),
    )
    out_specs = (P("group", "blk", None), P("group", "blk", None, None, None))
    return jax.shard_map(shards, mesh=mesh, in_specs=in_specs, out_specs=out_specs, check_vma=False)
```

```python
import functools

import jax
import jax.numpy as jnp
from jax import lax
from jax.experimental import pallas as pl
from jax.experimental.pallas import tpu as pltpu
from jax.sharding import PartitionSpec as P


CAP = 4
PLANE = 8
LAG = 2


FIRST_LIMIT = 62_500_000

learn_rate = 0.01
shrinkage = 0.05

VMEM = pl.BlockSpec(memory_space=pltpu.VMEM)
SMEM = pl.BlockSpec(memory_space=pltpu.SMEM)
ANY = pl.BlockSpec(memory_space=pl.ANY)
HBM = pl.BlockSpec(memory_space=pltpu.MemorySpace.HBM)
F32 = jnp.float32
BF16 = jnp.bfloat16


def call(
    body, out_shape, in_specs, out_specs, scratch=(), flops=0, moved=1 << 20, alias={},
    limit=12 << 20,
):
    return pl.pallas_call(
        body,
        out_shape=out_shape,
        in_specs=in_specs,
        out_specs=out_specs,
        scratch_shapes=scratch,
        input_output_aliases=alias,
        cost_estimate=pl.CostEstimate(flops=flops, bytes_accessed=moved, transcendentals=0),
        compiler_params=pltpu.CompilerParams(vmem_limit_bytes=limit),
    )


def stop_at(slot, inner, stops):
    if slot <= inner and slot < stops:
        return slot
    return slot - LAG if inner + LAG < slot < stops + LAG else None


def plan_slot(slot, stops, count_ref):
    inner = lax.rem(lax.axis_index("blk"), PLANE)
    early = jnp.logical_and(slot <= inner, slot < stops)
    late = jnp.logical_and(slot > inner + LAG, slot < stops + LAG)
    active = jnp.logical_or(early, late)
    stop = jnp.clip(jnp.where(late, slot - LAG, slot), 0, stops - 1)
    count = jnp.where(active, count_ref[stop], 0)
    crossed = jnp.logical_and(late, inner == 0)
    return active, stop, count, crossed


def fetch(stop, count, row_ref, user_ref, low_ref, rated_ref, tiles, copy):
    tile = tiles.shape[1]
    for c in range(tiles.shape[0]):
        rows = pl.ds(c * tile, tile)

        @pl.when(c < count)
        def _():
            first = pl.multiple_of(row_ref[c, stop] * tile, tile)
            low_ref[rows, :] = user_ref[pl.ds(first, tile), :].astype(BF16)

        @pl.when(c >= count)
        def _():
            low_ref[rows, :] = jnp.zeros((tile, low_ref.shape[1]), BF16)
            rated_ref[:, rows] = jnp.zeros((rated_ref.shape[0], tile), BF16)

    copy.wait()
    for c in range(tiles.shape[0]):
        rows = pl.ds(c * tile, tile)

        @pl.when(c < count)
        def _():
            rated_ref[:, rows] = tiles[c].T


def update_items(exact, item_low, count, low_ref, rated_ref, residual_ref, item_ref):
    item_ref[...] = item_low
    tile = item_ref.shape[0]
    grad = None
    for c in range(low_ref.shape[0] // tile):
        span = slice(c * tile, (c + 1) * tile)
        low = low_ref[span, :]
        predicted = lax.dot_general(
            item_low, low, (((1,), (1,)), ((), ())), preferred_element_type=F32
        )
        residual = (rated_ref[:, span].astype(F32) - predicted).astype(BF16)
        residual_ref[:, span] = residual
        part = jnp.dot(residual, low, preferred_element_type=F32)
        grad = part if grad is None else grad + part
    decay = shrinkage * count.astype(F32)
    return (exact + learn_rate * (grad - decay * exact)).astype(BF16)


def first_body(
    count_hbm, row_hbm, user_hbm, item_hbm, ratings_hbm, next_ref, residual_ref, item_ref,
    count_ref, row_ref, user_ref, exact_ref, tiles, low_ref, rated_ref, sems,
):
    pairs = [
        (count_hbm, count_ref),
        (row_hbm, row_ref),
        (user_hbm, user_ref),
        (item_hbm, exact_ref),
        (ratings_hbm.at[0], tiles),
    ]
    moves = [pltpu.make_async_copy(*pair, sems.at[n]) for n, pair in enumerate(pairs)]
    for move in moves:
        move.start()
    for move in moves[:3]:
        move.wait()
    count = count_ref[0]
    fetch(0, count, row_ref, user_ref, low_ref, rated_ref, tiles, moves[4])
    moves[3].wait()
    exact = exact_ref[...]
    next_ref[...] = update_items(
        exact, exact.astype(BF16), count, low_ref, rated_ref, residual_ref, item_ref
    )


def item_body(slot, stops, last, n_in, count_ref, *refs):
    sources = refs[:n_in]
    low_ref, rated_ref, next_ref, residual_ref, item_ref = refs[n_in:]
    active, _, count, crossed = plan_slot(slot, stops, count_ref)

    def emit(block):
        if last:
            groups, halves, rows, columns = next_ref.shape
            for h in range(halves):
                half = block[:, h * columns : (h + 1) * columns]
                next_ref[:, h] = half.reshape(groups, rows, columns)
        else:
            next_ref[...] = block

    @pl.when(active)
    def _():
        item_low = sources[0][...]
        if n_in == 3:
            item_low = jnp.where(crossed, sources[2][...], item_low)
        exact = item_low.astype(F32)
        emit(update_items(exact, item_low, count, low_ref, rated_ref, residual_ref, item_ref))

    @pl.when(jnp.logical_not(active))
    def _():
        emit(sources[1][...])


def user_body(slot, stops, last, count_ref, row_ref, residual_ref, item_ref, user_ref, *refs):
    _, stop, count, _ = plan_slot(slot, stops, count_ref)
    if last:
        (out_ref,) = refs
    else:
        ratings_ref, out_ref, low_ref, rated_ref, tiles, sem = refs
        next_active, next_stop, next_count, _ = plan_slot(slot + 1, stops, count_ref)
        copy = pltpu.make_async_copy(ratings_ref.at[next_stop], tiles, sem)
        pl.when(next_active)(copy.start)
    tile = item_ref.shape[0]
    out_ref[...] = user_ref[...]
    for c in range(residual_ref.shape[1] // tile):

        @pl.when(c < count)
        def _():
            step = lax.dot_general(
                residual_ref[:, c * tile : (c + 1) * tile],
                item_ref[...],
                (((0,), (0,)), ((), ())),
                preferred_element_type=F32,
            )
            rows = pl.ds(pl.multiple_of(row_ref[c, stop] * tile, tile), tile)
            before = user_ref[rows, :]
            out_ref[rows, :] = before + learn_rate * (step - shrinkage * before)

    if not last:

        @pl.when(next_active)
        def _():
            fetch(next_stop, next_count, row_ref, out_ref, low_ref, rated_ref, tiles, copy)


def route_body(stops, plan_ref, index_ref, filled):
    groups, blocks = plan_ref.shape
    group = lax.rem(lax.axis_index("group") + groups - 1, groups)

    @pl.loop(0, blocks)
    def _(d):
        filled[d] = 0
        for c in range(CAP):
            index_ref[d * CAP + c] = blocks

    @pl.loop(0, blocks)
    def _(k):
        dest = plan_ref[group, k]
        place = filled[dest]
        filled[dest] = place + 1
        index_ref[dest * CAP + place] = lax.rem(k + (stops - 1), blocks)


def pick_body(index_ref, pieces_ref, out_ref, held):
    blocks = pieces_ref.shape[0]
    held[pl.ds(0, blocks)] = pieces_ref[...]
    held[blocks] = jnp.zeros(held.shape[1:], held.dtype)

    @pl.loop(0, out_ref.shape[0], unroll=16)
    def _(d):
        for c in range(CAP):
            out_ref[d, c] = held[index_ref[d * CAP + c]]


def place_body(pieces_ref, out_ref):
    groups, halves, slots, rows, columns = pieces_ref.shape
    for c in range(slots):
        for h in range(halves):
            out_ref[c, :, h * columns : (h + 1) * columns] = pieces_ref[:, h, c].reshape(
                groups * rows, columns
            )


def shards(user_factors, item_factors, ratings, tile_rows, counts, plan):
    users = user_factors[0]
    rating_tiles = ratings[0, 0]
    row_table = tile_rows[0, 0].T
    count_table = counts[0, 0]
    stops, tiles_at_stop, tile, _ = rating_tiles.shape
    blocks = lax.axis_size("blk")
    groups = lax.axis_size("group")
    items, rank = item_factors.shape[1:]
    wide = tiles_at_stop * tile
    slots = stops + LAG

    low_shape = jax.ShapeDtypeStruct((wide, rank), BF16)
    rated_shape = jax.ShapeDtypeStruct((items, wide), BF16)
    block_shape = jax.ShapeDtypeStruct((items, rank), BF16)
    piece_shape = jax.ShapeDtypeStruct((items // 8, rank // 128, 8, 128), BF16)
    user_shape = jax.ShapeDtypeStruct(users.shape, F32)
    tile_scratch = [pltpu.VMEM((tiles_at_stop, tile, tile), BF16), pltpu.SemaphoreType.DMA]
    block, residual, item_low = call(
        first_body,
        (block_shape, rated_shape, block_shape),
        [HBM] * 5,
        (VMEM, VMEM, VMEM),
        [
            pltpu.SMEM(count_table.shape, jnp.int32),
            pltpu.SMEM(row_table.shape, jnp.int32),
            pltpu.VMEM(users.shape, F32),
            pltpu.VMEM((items, rank), F32),
            tile_scratch[0],
            pltpu.VMEM(low_shape.shape, BF16),
            pltpu.VMEM(rated_shape.shape, BF16),
            pltpu.SemaphoreType.DMA((5,)),
        ],
        4 * items * wide * rank,
        limit=FIRST_LIMIT,
    )(count_table, row_table, users, item_factors[0], rating_tiles)

    across = [(b, (b + 1) % blocks) for b in range(PLANE - 1, blocks, PLANE)]
    crossing = {}
    for slot in range(slots):
        last = slot == slots - 1
        if slot > 0:
            block, residual, item_low = call(
                functools.partial(item_body, slot, stops, last, len(arrived)),
                (piece_shape if last else block_shape, rated_shape, block_shape),
                [SMEM] + [VMEM] * (len(arrived) + 2),
                (VMEM, VMEM, VMEM),
                (),
                4 * items * wide * rank,
            )(count_table, *arrived, low, rated)
        if not last:
            within = [
                (b, b + 1)
                for b in range(blocks)
                if b % PLANE != PLANE - 1
                and stop_at(slot, b % PLANE, stops) is not None
                and stop_at(slot + 1, b % PLANE + 1, stops) == stop_at(slot, b % PLANE, stops) + 1
            ]
            arrived = [lax.ppermute(block, "blk", within), block]
            if slot < stops - 1:
                crossing[slot + 1 + LAG] = lax.ppermute(block, "blk", across)
            if slot + 1 in crossing:
                arrived.append(crossing[slot + 1])
        body = functools.partial(user_body, slot, stops, last)
        operands = (count_table, row_table, residual, item_low, users)
        flops = 2 * wide * items * rank
        if last:
            users = call(
                body, user_shape, [SMEM, SMEM, VMEM, VMEM, VMEM], VMEM, (), flops
            )(*operands)
        else:
            users, low, rated = call(
                body,
                (user_shape, low_shape, rated_shape),
                [SMEM, SMEM, VMEM, VMEM, VMEM, ANY],
                (VMEM, VMEM, VMEM),
                tile_scratch,
                flops,
                alias={4: 0} if slot else {},
            )(*operands, rating_tiles)

    pieces = block.reshape(blocks, -1, 128)
    index = call(
        functools.partial(route_body, stops),
        jax.ShapeDtypeStruct((blocks * CAP,), jnp.int32),
        [SMEM],
        SMEM,
        [pltpu.SMEM((blocks,), jnp.int32)],
        moved=4 * blocks,
    )(plan)
    shifted = lax.ppermute(pieces, "group", [(g, (g + 1) % groups) for g in range(groups)])
    spread = lax.all_to_all(shifted, "blk", split_axis=0, concat_axis=0, tiled=True)
    picked = call(
        pick_body,
        jax.ShapeDtypeStruct((blocks, CAP) + pieces.shape[1:], BF16),
        [SMEM, VMEM],
        VMEM,
        [pltpu.VMEM((blocks + 1,) + pieces.shape[1:], BF16)],
    )(index, spread)
    landed = lax.all_to_all(picked, "blk", split_axis=0, concat_axis=0, tiled=True)
    landed = landed.reshape(blocks, CAP, -1, 8, 128).transpose(0, 2, 1, 3, 4)
    received = call(
        place_body, jax.ShapeDtypeStruct((CAP, items, rank), BF16), [VMEM], VMEM
    )(landed.reshape(items // 8, rank // 128, CAP, 8, 128))
    return (users[None], received[None, None])


def solution(mesh):
    in_specs = (
        P("group", "blk", None),
        P("group", "blk", None),
        P("group", "blk", None, None, None, None),
        P("group", "blk", None, None),
        P("group", "blk", None),
        P(),
    )
    out_specs = (P("group", "blk", None), P("group", "blk", None, None, None))
    return jax.shard_map(shards, mesh=mesh, in_specs=in_specs, out_specs=out_specs, check_vma=False)
```

```python
import functools

import jax
import jax.numpy as jnp
from jax import lax
from jax.experimental import pallas as pl
from jax.experimental.pallas import tpu as pltpu
from jax.sharding import PartitionSpec as P


CAP = 4
PLANE = 8
GROUP_ROW = 4
LAG = 2


FIRST_LIMIT = 62_500_000

learn_rate = 0.01
shrinkage = 0.05

VMEM = pl.BlockSpec(memory_space=pltpu.VMEM)
SMEM = pl.BlockSpec(memory_space=pltpu.SMEM)
ANY = pl.BlockSpec(memory_space=pl.ANY)
HBM = pl.BlockSpec(memory_space=pltpu.MemorySpace.HBM)
F32 = jnp.float32
BF16 = jnp.bfloat16


def call(
    body, out_shape, in_specs, out_specs, scratch=(), flops=0, moved=1 << 20, alias={},
    limit=12 << 20,
):
    return pl.pallas_call(
        body,
        out_shape=out_shape,
        in_specs=in_specs,
        out_specs=out_specs,
        scratch_shapes=scratch,
        input_output_aliases=alias,
        cost_estimate=pl.CostEstimate(flops=flops, bytes_accessed=moved, transcendentals=0),
        compiler_params=pltpu.CompilerParams(vmem_limit_bytes=limit),
    )


def hand_over(position, group, blocks, groups):
    if group % GROUP_ROW == GROUP_ROW - 1:
        plane, inner = divmod(position, PLANE)
        position = (blocks // PLANE - 1 - plane) * PLANE + inner
    return position, (group + 1) % groups


def stop_at(slot, inner, stops):
    if slot <= inner and slot < stops:
        return slot
    return slot - LAG if inner + LAG < slot < stops + LAG else None


def plan_slot(slot, stops, count_ref):
    inner = lax.rem(lax.axis_index("blk"), PLANE)
    early = jnp.logical_and(slot <= inner, slot < stops)
    late = jnp.logical_and(slot > inner + LAG, slot < stops + LAG)
    active = jnp.logical_or(early, late)
    stop = jnp.clip(jnp.where(late, slot - LAG, slot), 0, stops - 1)
    count = jnp.where(active, count_ref[stop], 0)
    crossed = jnp.logical_and(late, inner == 0)
    return active, stop, count, crossed


def fetch(stop, count, row_ref, user_ref, low_ref, rated_ref, tiles, copy):
    tile = tiles.shape[1]
    for c in range(tiles.shape[0]):
        rows = pl.ds(c * tile, tile)

        @pl.when(c < count)
        def _():
            first = pl.multiple_of(row_ref[c, stop] * tile, tile)
            low_ref[rows, :] = user_ref[pl.ds(first, tile), :].astype(BF16)

        @pl.when(c >= count)
        def _():
            low_ref[rows, :] = jnp.zeros((tile, low_ref.shape[1]), BF16)
            rated_ref[:, rows] = jnp.zeros((rated_ref.shape[0], tile), BF16)

    copy.wait()
    for c in range(tiles.shape[0]):
        rows = pl.ds(c * tile, tile)

        @pl.when(c < count)
        def _():
            rated_ref[:, rows] = tiles[c].T


def update_items(exact, item_low, count, low_ref, rated_ref, residual_ref, item_ref):
    item_ref[...] = item_low
    tile = item_ref.shape[0]
    grad = None
    for c in range(low_ref.shape[0] // tile):
        span = slice(c * tile, (c + 1) * tile)
        low = low_ref[span, :]
        predicted = lax.dot_general(
            item_low, low, (((1,), (1,)), ((), ())), preferred_element_type=F32
        )
        residual = (rated_ref[:, span].astype(F32) - predicted).astype(BF16)
        residual_ref[:, span] = residual
        part = jnp.dot(residual, low, preferred_element_type=F32)
        grad = part if grad is None else grad + part
    decay = shrinkage * count.astype(F32)
    return (exact + learn_rate * (grad - decay * exact)).astype(BF16)


def first_body(
    count_hbm, row_hbm, user_hbm, item_hbm, ratings_hbm, next_ref, residual_ref, item_ref,
    count_ref, row_ref, user_ref, exact_ref, tiles, low_ref, rated_ref, sems,
):
    pairs = [
        (count_hbm, count_ref),
        (row_hbm, row_ref),
        (user_hbm, user_ref),
        (item_hbm, exact_ref),
        (ratings_hbm.at[0], tiles),
    ]
    moves = [pltpu.make_async_copy(*pair, sems.at[n]) for n, pair in enumerate(pairs)]
    for move in moves:
        move.start()
    for move in moves[:3]:
        move.wait()
    count = count_ref[0]
    fetch(0, count, row_ref, user_ref, low_ref, rated_ref, tiles, moves[4])
    moves[3].wait()
    exact = exact_ref[...]
    next_ref[...] = update_items(
        exact, exact.astype(BF16), count, low_ref, rated_ref, residual_ref, item_ref
    )


def item_body(slot, stops, last, n_in, count_ref, *refs):
    sources = refs[:n_in]
    low_ref, rated_ref, next_ref, residual_ref, item_ref = refs[n_in:]
    active, _, count, crossed = plan_slot(slot, stops, count_ref)

    def emit(block):
        if last:
            groups, halves, rows, columns = next_ref.shape
            for h in range(halves):
                half = block[:, h * columns : (h + 1) * columns]
                next_ref[:, h] = half.reshape(groups, rows, columns)
        else:
            next_ref[...] = block

    @pl.when(active)
    def _():
        item_low = sources[0][...]
        if n_in == 3:
            item_low = jnp.where(crossed, sources[2][...], item_low)
        exact = item_low.astype(F32)
        emit(update_items(exact, item_low, count, low_ref, rated_ref, residual_ref, item_ref))

    @pl.when(jnp.logical_not(active))
    def _():
        emit(sources[1][...])


def user_body(slot, stops, last, count_ref, row_ref, residual_ref, item_ref, user_ref, *refs):
    _, stop, count, _ = plan_slot(slot, stops, count_ref)
    if last:
        (out_ref,) = refs
    else:
        ratings_ref, out_ref, low_ref, rated_ref, tiles, sem = refs
        next_active, next_stop, next_count, _ = plan_slot(slot + 1, stops, count_ref)
        copy = pltpu.make_async_copy(ratings_ref.at[next_stop], tiles, sem)
        pl.when(next_active)(copy.start)
    tile = item_ref.shape[0]
    out_ref[...] = user_ref[...]
    for c in range(residual_ref.shape[1] // tile):

        @pl.when(c < count)
        def _():
            step = lax.dot_general(
                residual_ref[:, c * tile : (c + 1) * tile],
                item_ref[...],
                (((0,), (0,)), ((), ())),
                preferred_element_type=F32,
            )
            rows = pl.ds(pl.multiple_of(row_ref[c, stop] * tile, tile), tile)
            before = user_ref[rows, :]
            out_ref[rows, :] = before + learn_rate * (step - shrinkage * before)

    if not last:

        @pl.when(next_active)
        def _():
            fetch(next_stop, next_count, row_ref, out_ref, low_ref, rated_ref, tiles, copy)


def route_body(stops, plan_ref, index_ref, filled):
    groups, blocks = plan_ref.shape
    group = lax.rem(lax.axis_index("group") + groups - 1, groups)
    turned = lax.rem(group, GROUP_ROW) == GROUP_ROW - 1

    @pl.loop(0, blocks)
    def _(d):
        filled[d] = 0
        for c in range(CAP):
            index_ref[d * CAP + c] = blocks

    @pl.loop(0, blocks)
    def _(k):
        dest = plan_ref[group, k]
        place = filled[dest]
        filled[dest] = place + 1
        at = lax.rem(k + (stops - 1), blocks)
        inner = lax.rem(at, PLANE)
        index_ref[dest * CAP + place] = jnp.where(turned, blocks - PLANE - at + 2 * inner, at)


def pick_body(index_ref, pieces_ref, out_ref, held):
    blocks = pieces_ref.shape[0]
    held[pl.ds(0, blocks)] = pieces_ref[...]
    held[blocks] = jnp.zeros(held.shape[1:], held.dtype)

    @pl.loop(0, out_ref.shape[0], unroll=16)
    def _(d):
        for c in range(CAP):
            out_ref[d, c] = held[index_ref[d * CAP + c]]


def place_body(pieces_ref, out_ref):
    groups, halves, slots, rows, columns = pieces_ref.shape
    for c in range(slots):
        for h in range(halves):
            out_ref[c, :, h * columns : (h + 1) * columns] = pieces_ref[:, h, c].reshape(
                groups * rows, columns
            )


def shards(user_factors, item_factors, ratings, tile_rows, counts, plan):
    users = user_factors[0]
    rating_tiles = ratings[0, 0]
    row_table = tile_rows[0, 0].T
    count_table = counts[0, 0]
    stops, tiles_at_stop, tile, _ = rating_tiles.shape
    blocks = lax.axis_size("blk")
    groups = lax.axis_size("group")
    items, rank = item_factors.shape[1:]
    wide = tiles_at_stop * tile
    slots = stops + LAG

    low_shape = jax.ShapeDtypeStruct((wide, rank), BF16)
    rated_shape = jax.ShapeDtypeStruct((items, wide), BF16)
    block_shape = jax.ShapeDtypeStruct((items, rank), BF16)
    piece_shape = jax.ShapeDtypeStruct((items // 8, rank // 128, 8, 128), BF16)
    user_shape = jax.ShapeDtypeStruct(users.shape, F32)
    tile_scratch = [pltpu.VMEM((tiles_at_stop, tile, tile), BF16), pltpu.SemaphoreType.DMA]
    block, residual, item_low = call(
        first_body,
        (block_shape, rated_shape, block_shape),
        [HBM] * 5,
        (VMEM, VMEM, VMEM),
        [
            pltpu.SMEM(count_table.shape, jnp.int32),
            pltpu.SMEM(row_table.shape, jnp.int32),
            pltpu.VMEM(users.shape, F32),
            pltpu.VMEM((items, rank), F32),
            tile_scratch[0],
            pltpu.VMEM(low_shape.shape, BF16),
            pltpu.VMEM(rated_shape.shape, BF16),
            pltpu.SemaphoreType.DMA((5,)),
        ],
        4 * items * wide * rank,
        limit=FIRST_LIMIT,
    )(count_table, row_table, users, item_factors[0], rating_tiles)

    across = [(b, (b + 1) % blocks) for b in range(PLANE - 1, blocks, PLANE)]
    crossing = {}
    for slot in range(slots):
        last = slot == slots - 1
        if slot > 0:
            block, residual, item_low = call(
                functools.partial(item_body, slot, stops, last, len(arrived)),
                (piece_shape if last else block_shape, rated_shape, block_shape),
                [SMEM] + [VMEM] * (len(arrived) + 2),
                (VMEM, VMEM, VMEM),
                (),
                4 * items * wide * rank,
            )(count_table, *arrived, low, rated)
        if not last:
            within = [
                (b, b + 1)
                for b in range(blocks)
                if b % PLANE != PLANE - 1
                and stop_at(slot, b % PLANE, stops) is not None
                and stop_at(slot + 1, b % PLANE + 1, stops) == stop_at(slot, b % PLANE, stops) + 1
            ]
            arrived = [lax.ppermute(block, "blk", within), block]
            if slot < stops - 1:
                crossing[slot + 1 + LAG] = lax.ppermute(block, "blk", across)
            if slot + 1 in crossing:
                arrived.append(crossing[slot + 1])
        body = functools.partial(user_body, slot, stops, last)
        operands = (count_table, row_table, residual, item_low, users)
        flops = 2 * wide * items * rank
        if last:
            users = call(
                body, user_shape, [SMEM, SMEM, VMEM, VMEM, VMEM], VMEM, (), flops
            )(*operands)
        else:
            users, low, rated = call(
                body,
                (user_shape, low_shape, rated_shape),
                [SMEM, SMEM, VMEM, VMEM, VMEM, ANY],
                (VMEM, VMEM, VMEM),
                tile_scratch,
                flops,
                alias={4: 0} if slot else {},
            )(*operands, rating_tiles)

    pieces = block.reshape(blocks, -1, 128)
    index = call(
        functools.partial(route_body, stops),
        jax.ShapeDtypeStruct((blocks * CAP,), jnp.int32),
        [SMEM],
        SMEM,
        [pltpu.SMEM((blocks,), jnp.int32)],
        moved=4 * blocks,
    )(plan)
    moves = []
    for b in range(blocks):
        for g in range(groups):
            to_b, to_g = hand_over(b, g, blocks, groups)
            moves.append((b * groups + g, to_b * groups + to_g))
    shifted = lax.ppermute(pieces, ("blk", "group"), moves)
    spread = lax.all_to_all(shifted, "blk", split_axis=0, concat_axis=0, tiled=True)
    picked = call(
        pick_body,
        jax.ShapeDtypeStruct((blocks, CAP) + pieces.shape[1:], BF16),
        [SMEM, VMEM],
        VMEM,
        [pltpu.VMEM((blocks + 1,) + pieces.shape[1:], BF16)],
    )(index, spread)
    landed = lax.all_to_all(picked, "blk", split_axis=0, concat_axis=0, tiled=True)
    landed = landed.reshape(blocks, CAP, -1, 8, 128).transpose(0, 2, 1, 3, 4)
    received = call(
        place_body, jax.ShapeDtypeStruct((CAP, items, rank), BF16), [VMEM], VMEM
    )(landed.reshape(items // 8, rank // 128, CAP, 8, 128))
    return (users[None], received[None, None])


def solution(mesh):
    in_specs = (
        P("group", "blk", None),
        P("group", "blk", None),
        P("group", "blk", None, None, None, None),
        P("group", "blk", None, None),
        P("group", "blk", None),
        P(),
    )
    out_specs = (P("group", "blk", None), P("group", "blk", None, None, None))
    return jax.shard_map(shards, mesh=mesh, in_specs=in_specs, out_specs=out_specs, check_vma=False)
```

```python
import functools

import jax
import jax.numpy as jnp
from jax import lax
from jax.experimental import pallas as pl
from jax.experimental.pallas import tpu as pltpu
from jax.sharding import PartitionSpec as P


CAP = 4
PLANE = 8
GROUP_ROW = 4
LAG = 2


FIRST_LIMIT = 62_500_000

learn_rate = 0.01
shrinkage = 0.05

VMEM = pl.BlockSpec(memory_space=pltpu.VMEM)
SMEM = pl.BlockSpec(memory_space=pltpu.SMEM)
ANY = pl.BlockSpec(memory_space=pl.ANY)
HBM = pl.BlockSpec(memory_space=pltpu.MemorySpace.HBM)
F32 = jnp.float32
BF16 = jnp.bfloat16


def call(
    body, out_shape, in_specs, out_specs, scratch=(), flops=0, moved=1 << 20, alias={},
    limit=12 << 20,
):
    return pl.pallas_call(
        body,
        out_shape=out_shape,
        in_specs=in_specs,
        out_specs=out_specs,
        scratch_shapes=scratch,
        input_output_aliases=alias,
        cost_estimate=pl.CostEstimate(flops=flops, bytes_accessed=moved, transcendentals=0),
        compiler_params=pltpu.CompilerParams(vmem_limit_bytes=limit),
    )


def hand_over(position, group, blocks, groups):
    if group % GROUP_ROW == GROUP_ROW - 1:
        plane, inner = divmod(position, PLANE)
        position = (blocks // PLANE - 1 - plane) * PLANE + inner
    return position, (group + 1) % groups


def stop_at(slot, inner, stops):
    if slot <= inner and slot < stops:
        return slot
    return slot - LAG if inner + LAG < slot < stops + LAG else None


def plan_slot(slot, stops):
    inner = lax.rem(lax.axis_index("blk"), PLANE)
    early = jnp.logical_and(slot <= inner, slot < stops)
    late = jnp.logical_and(slot > inner + LAG, slot < stops + LAG)
    active = jnp.logical_or(early, late)
    stop = jnp.clip(jnp.where(late, slot - LAG, slot), 0, stops - 1)
    return active, stop, jnp.logical_and(late, inner == 0), lax.rem(inner, 2)


def fetch(stop, count, row_ref, user_ref, low_ref, rated_ref, tiles, copy):
    tile = tiles.shape[1]
    for c in range(tiles.shape[0]):
        rows = pl.ds(c * tile, tile)

        @pl.when(c < count)
        def _():
            first = pl.multiple_of(row_ref[c, stop] * tile, tile)
            low_ref[rows, :] = user_ref[pl.ds(first, tile), :].astype(BF16)

        @pl.when(c >= count)
        def _():
            low_ref[rows, :] = jnp.zeros((tile, low_ref.shape[1]), BF16)
            rated_ref[:, rows] = jnp.zeros((rated_ref.shape[0], tile), BF16)

    copy.wait()
    for c in range(tiles.shape[0]):
        rows = pl.ds(c * tile, tile)

        @pl.when(c < count)
        def _():
            rated_ref[:, rows] = tiles[c].T


def update_items(exact, item_low, decay, low_ref, rated_ref, residual_ref, item_ref):
    item_ref[...] = item_low
    tile = item_ref.shape[0]
    grad = None
    for c in range(low_ref.shape[0] // tile):
        span = slice(c * tile, (c + 1) * tile)
        low = low_ref[span, :]
        predicted = lax.dot_general(
            item_low, low, (((1,), (1,)), ((), ())), preferred_element_type=F32
        )
        residual = (rated_ref[:, span].astype(F32) - predicted).astype(BF16)
        residual_ref[:, span] = residual
        part = jnp.dot(residual, low, preferred_element_type=F32)
        grad = part if grad is None else grad + part
    return (exact + learn_rate * (grad - decay * exact)).astype(BF16)


def first_body(
    count_hbm, row_hbm, user_hbm, item_hbm, ratings_hbm, next_ref, residual_ref, item_ref,
    count_ref, row_ref, user_ref, exact_ref, tiles, low_ref, rated_ref, sems,
):
    pairs = [
        (count_hbm, count_ref),
        (row_hbm, row_ref),
        (user_hbm, user_ref),
        (item_hbm, exact_ref),
        (ratings_hbm.at[0], tiles),
    ]
    moves = [pltpu.make_async_copy(*pair, sems.at[n]) for n, pair in enumerate(pairs)]
    for move in moves:
        move.start()
    for move in moves[:3]:
        move.wait()
    count = count_ref[0]
    fetch(0, count, row_ref, user_ref, low_ref, rated_ref, tiles, moves[4])
    moves[3].wait()
    exact = exact_ref[...]
    next_ref[...] = update_items(
        exact, exact.astype(BF16), shrinkage * count.astype(F32), low_ref, rated_ref,
        residual_ref, item_ref,
    )


def item_body(slot, stops, parity, last, arrivals, *refs):
    sources = refs[:arrivals]
    held_ref, low_ref, rated_ref, decay_ref = refs[arrivals : arrivals + 4]
    others = refs[arrivals + 4 : -3]
    next_ref, residual_ref, item_ref = refs[-3:]
    active, _, crossed, own = plan_slot(slot, stops)

    def emit(block):
        if last:
            groups, halves, rows, columns = next_ref.shape
            for h in range(halves):
                half = block[:, h * columns : (h + 1) * columns]
                next_ref[:, h] = half.reshape(groups, rows, columns)
        else:
            next_ref[...] = block

    @pl.when(jnp.logical_and(own == parity, active))
    def _():
        item_low = sources[0][...]
        if arrivals == 2:
            item_low = jnp.where(crossed, sources[1][...], item_low)
        emit(
            update_items(
                item_low.astype(F32), item_low, decay_ref[0:1, :], low_ref, rated_ref,
                residual_ref, item_ref,
            )
        )

    @pl.when(jnp.logical_and(own == parity, jnp.logical_not(active)))
    def _():
        emit(held_ref[...])

    if others:

        @pl.when(own != parity)
        def _():
            emit(others[0][...])
            residual_ref[...] = others[1][...]
            item_ref[...] = others[2][...]


def user_body(slot, stops, last, count_ref, row_ref, residual_ref, item_ref, user_ref, *refs):
    active, stop, _, _ = plan_slot(slot, stops)
    count = jnp.where(active, count_ref[stop], 0)
    if last:
        (out_ref,) = refs
    else:
        ratings_ref, out_ref, low_ref, rated_ref, decay_ref, tiles, sem = refs
        next_active, next_stop, _, _ = plan_slot(slot + 1, stops)
        next_count = jnp.where(next_active, count_ref[next_stop], 0)
        decay_ref[...] = jnp.full(decay_ref.shape, shrinkage * next_count.astype(F32))
        copy = pltpu.make_async_copy(ratings_ref.at[next_stop], tiles, sem)
        pl.when(next_active)(copy.start)
    tile = item_ref.shape[0]
    out_ref[...] = user_ref[...]
    for c in range(residual_ref.shape[1] // tile):

        @pl.when(c < count)
        def _():
            step = lax.dot_general(
                residual_ref[:, c * tile : (c + 1) * tile],
                item_ref[...],
                (((0,), (0,)), ((), ())),
                preferred_element_type=F32,
            )
            rows = pl.ds(pl.multiple_of(row_ref[c, stop] * tile, tile), tile)
            before = user_ref[rows, :]
            out_ref[rows, :] = before + learn_rate * (step - shrinkage * before)

    if not last:

        @pl.when(next_active)
        def _():
            fetch(next_stop, next_count, row_ref, out_ref, low_ref, rated_ref, tiles, copy)


def route_body(stops, plan_ref, index_ref, filled):
    groups, blocks = plan_ref.shape
    group = lax.rem(lax.axis_index("group") + groups - 1, groups)
    turned = lax.rem(group, GROUP_ROW) == GROUP_ROW - 1

    @pl.loop(0, blocks)
    def _(d):
        filled[d] = 0
        for c in range(CAP):
            index_ref[d * CAP + c] = blocks

    @pl.loop(0, blocks)
    def _(k):
        dest = plan_ref[group, k]
        place = filled[dest]
        filled[dest] = place + 1
        at = lax.rem(k + (stops - 1), blocks)
        inner = lax.rem(at, PLANE)
        index_ref[dest * CAP + place] = jnp.where(turned, blocks - PLANE - at + 2 * inner, at)


def pick_body(index_ref, pieces_ref, out_ref, held):
    blocks = pieces_ref.shape[0]
    held[pl.ds(0, blocks)] = pieces_ref[...]
    held[blocks] = jnp.zeros(held.shape[1:], held.dtype)

    @pl.loop(0, out_ref.shape[0], unroll=16)
    def _(d):
        for c in range(CAP):
            out_ref[d, c] = held[index_ref[d * CAP + c]]


def place_body(pieces_ref, out_ref):
    groups, halves, slots, rows, columns = pieces_ref.shape
    for c in range(slots):
        for h in range(halves):
            out_ref[c, :, h * columns : (h + 1) * columns] = pieces_ref[:, h, c].reshape(
                groups * rows, columns
            )


def shards(user_factors, item_factors, ratings, tile_rows, counts, plan):
    users = user_factors[0]
    rating_tiles = ratings[0, 0]
    row_table = tile_rows[0, 0].T
    count_table = counts[0, 0]
    stops, tiles_at_stop, tile, _ = rating_tiles.shape
    blocks = lax.axis_size("blk")
    groups = lax.axis_size("group")
    items, rank = item_factors.shape[1:]
    wide = tiles_at_stop * tile
    slots = stops + LAG

    low_shape = jax.ShapeDtypeStruct((wide, rank), BF16)
    rated_shape = jax.ShapeDtypeStruct((items, wide), BF16)
    block_shape = jax.ShapeDtypeStruct((items, rank), BF16)
    decay_shape = jax.ShapeDtypeStruct((8, rank), F32)
    piece_shape = jax.ShapeDtypeStruct((items // 8, rank // 128, 8, 128), BF16)
    user_shape = jax.ShapeDtypeStruct(users.shape, F32)
    tile_scratch = [pltpu.VMEM((tiles_at_stop, tile, tile), BF16), pltpu.SemaphoreType.DMA]
    block, residual, item_low = call(
        first_body,
        (block_shape, rated_shape, block_shape),
        [HBM] * 5,
        (VMEM, VMEM, VMEM),
        [
            pltpu.SMEM(count_table.shape, jnp.int32),
            pltpu.SMEM(row_table.shape, jnp.int32),
            pltpu.VMEM(users.shape, F32),
            pltpu.VMEM((items, rank), F32),
            tile_scratch[0],
            pltpu.VMEM(low_shape.shape, BF16),
            pltpu.VMEM(rated_shape.shape, BF16),
            pltpu.SemaphoreType.DMA((5,)),
        ],
        4 * items * wide * rank,
        limit=FIRST_LIMIT,
    )(count_table, row_table, users, item_factors[0], rating_tiles)

    across = [(b, (b + 1) % blocks) for b in range(PLANE - 1, blocks, PLANE)]

    def within(slot, parity):
        pairs = []
        for b in range(blocks):
            inner = b % PLANE
            if inner % 2 == parity and inner != PLANE - 1:
                here, there = stop_at(slot, inner, stops), stop_at(slot + 1, inner + 1, stops)
                if here is not None and there == here + 1:
                    pairs.append((b, b + 1))
        return pairs

    odd_block = block
    from_odd = from_even = None
    crossing = {}
    for slot in range(slots):
        last = slot == slots - 1

        def items_call(parity, arrived, others):
            ends = last and parity == 0
            return call(
                functools.partial(item_body, slot, stops, parity, ends, len(arrived)),
                (piece_shape if ends else block_shape, rated_shape, block_shape),
                [VMEM] * (len(arrived) + 4 + len(others)),
                (VMEM, VMEM, VMEM),
                (),
                2 * items * wide * rank,
            )(*arrived, block, low, rated, decay, *others)

        if slot > 0:
            others = items_call(1, [from_even], ())
            odd_block = others[0]
        arrived = [from_odd] + ([crossing[slot]] if slot in crossing else [])
        if not last:
            from_odd = lax.ppermute(odd_block, "blk", within(slot, 1))
        if slot < stops - 1:
            crossing[slot + 1 + LAG] = lax.ppermute(odd_block, "blk", across)
        if slot > 0:
            block, residual, item_low = items_call(0, arrived, others)
        if not last:
            from_even = lax.ppermute(block, "blk", within(slot, 0))
        body = functools.partial(user_body, slot, stops, last)
        operands = (count_table, row_table, residual, item_low, users)
        flops = 2 * wide * items * rank
        if last:
            users = call(
                body, user_shape, [SMEM, SMEM, VMEM, VMEM, VMEM], VMEM, (), flops
            )(*operands)
        else:
            users, low, rated, decay = call(
                body,
                (user_shape, low_shape, rated_shape, decay_shape),
                [SMEM, SMEM, VMEM, VMEM, VMEM, ANY],
                (VMEM, VMEM, VMEM, VMEM),
                tile_scratch,
                flops,
                alias={4: 0} if slot else {},
            )(*operands, rating_tiles)

    pieces = block.reshape(blocks, -1, 128)
    index = call(
        functools.partial(route_body, stops),
        jax.ShapeDtypeStruct((blocks * CAP,), jnp.int32),
        [SMEM],
        SMEM,
        [pltpu.SMEM((blocks,), jnp.int32)],
        moved=4 * blocks,
    )(plan)
    moves = []
    for b in range(blocks):
        for g in range(groups):
            to_b, to_g = hand_over(b, g, blocks, groups)
            moves.append((b * groups + g, to_b * groups + to_g))
    shifted = lax.ppermute(pieces, ("blk", "group"), moves)
    spread = lax.all_to_all(shifted, "blk", split_axis=0, concat_axis=0, tiled=True)
    picked = call(
        pick_body,
        jax.ShapeDtypeStruct((blocks, CAP) + pieces.shape[1:], BF16),
        [SMEM, VMEM],
        VMEM,
        [pltpu.VMEM((blocks + 1,) + pieces.shape[1:], BF16)],
    )(index, spread)
    landed = lax.all_to_all(picked, "blk", split_axis=0, concat_axis=0, tiled=True)
    landed = landed.reshape(blocks, CAP, -1, 8, 128).transpose(0, 2, 1, 3, 4)
    received = call(
        place_body, jax.ShapeDtypeStruct((CAP, items, rank), BF16), [VMEM], VMEM
    )(landed.reshape(items // 8, rank // 128, CAP, 8, 128))
    return (users[None], received[None, None])


def solution(mesh):
    in_specs = (
        P("group", "blk", None),
        P("group", "blk", None),
        P("group", "blk", None, None, None, None),
        P("group", "blk", None, None),
        P("group", "blk", None),
        P(),
    )
    out_specs = (P("group", "blk", None), P("group", "blk", None, None, None))
    return jax.shard_map(shards, mesh=mesh, in_specs=in_specs, out_specs=out_specs, check_vma=False)
```

```python
import functools

import jax
import jax.numpy as jnp
from jax import lax
from jax.experimental import pallas as pl
from jax.experimental.pallas import tpu as pltpu
from jax.sharding import PartitionSpec as P


CAP = 4
PLANE = 8
GROUP_ROW = 4
LAG = 2


FIRST_LIMIT = 62_500_000

learn_rate = 0.01
shrinkage = 0.05

VMEM = pl.BlockSpec(memory_space=pltpu.VMEM)
SMEM = pl.BlockSpec(memory_space=pltpu.SMEM)
ANY = pl.BlockSpec(memory_space=pl.ANY)
HBM = pl.BlockSpec(memory_space=pltpu.MemorySpace.HBM)
F32 = jnp.float32
BF16 = jnp.bfloat16


def call(
    body, out_shape, in_specs, out_specs, scratch=(), flops=0, moved=1 << 20, alias={},
    limit=12 << 20,
):
    return pl.pallas_call(
        body,
        out_shape=out_shape,
        in_specs=in_specs,
        out_specs=out_specs,
        scratch_shapes=scratch,
        input_output_aliases=alias,
        cost_estimate=pl.CostEstimate(flops=flops, bytes_accessed=moved, transcendentals=0),
        compiler_params=pltpu.CompilerParams(vmem_limit_bytes=limit),
    )


def hand_over(position, group, blocks, groups):
    if group % GROUP_ROW == GROUP_ROW - 1:
        plane, inner = divmod(position, PLANE)
        position = (blocks // PLANE - 1 - plane) * PLANE + inner
    return position, (group + 1) % groups


def stop_at(slot, inner, stops):
    if slot <= inner and slot < stops:
        return slot
    return slot - LAG if inner + LAG < slot < stops + LAG else None


def plan_slot(slot, stops):
    inner = lax.rem(lax.axis_index("blk"), PLANE)
    early = jnp.logical_and(slot <= inner, slot < stops)
    late = jnp.logical_and(slot > inner + LAG, slot < stops + LAG)
    active = jnp.logical_or(early, late)
    stop = jnp.clip(jnp.where(late, slot - LAG, slot), 0, stops - 1)
    return active, stop, jnp.logical_and(late, inner == 0), lax.rem(inner, 2)


def fetch(stop, count, row_ref, user_ref, low_ref, rated_ref, tiles, copy=None):
    tile = tiles.shape[-1]
    for c in range(tiles.shape[-3]):
        rows = pl.ds(c * tile, tile)

        @pl.when(c < count)
        def _():
            first = pl.multiple_of(row_ref[c, stop] * tile, tile)
            low_ref[rows, :] = user_ref[pl.ds(first, tile), :].astype(BF16)

        @pl.when(c >= count)
        def _():
            low_ref[rows, :] = jnp.zeros((tile, low_ref.shape[1]), BF16)
            rated_ref[:, rows] = jnp.zeros((rated_ref.shape[0], tile), BF16)

    if copy is not None:
        copy.wait()
    for c in range(tiles.shape[-3]):
        rows = pl.ds(c * tile, tile)

        @pl.when(c < count)
        def _():
            rated_ref[:, rows] = (tiles[c] if copy is not None else tiles[stop, c]).T


def update_items(exact, item_low, decay, low_ref, rated_ref, residual_ref, item_ref):
    item_ref[...] = item_low
    tile = item_ref.shape[0]
    grad = None
    for c in range(low_ref.shape[0] // tile):
        span = slice(c * tile, (c + 1) * tile)
        low = low_ref[span, :]
        predicted = lax.dot_general(
            item_low, low, (((1,), (1,)), ((), ())), preferred_element_type=F32
        )
        residual = (rated_ref[:, span].astype(F32) - predicted).astype(BF16)
        residual_ref[:, span] = residual
        part = jnp.dot(residual, low, preferred_element_type=F32)
        grad = part if grad is None else grad + part
    return (exact + learn_rate * (grad - decay * exact)).astype(BF16)


def first_body(
    count_hbm, row_hbm, user_hbm, item_hbm, ratings_hbm, next_ref, residual_ref, item_ref,
    count_ref, row_ref, user_ref, exact_ref, tiles, low_ref, rated_ref, sems,
):
    pairs = [
        (count_hbm, count_ref),
        (row_hbm, row_ref),
        (user_hbm, user_ref),
        (item_hbm, exact_ref),
        (ratings_hbm.at[0], tiles),
    ]
    moves = [pltpu.make_async_copy(*pair, sems.at[n]) for n, pair in enumerate(pairs)]
    for move in moves:
        move.start()
    for move in moves[:3]:
        move.wait()
    count = count_ref[0]
    fetch(0, count, row_ref, user_ref, low_ref, rated_ref, tiles, moves[4])
    moves[3].wait()
    exact = exact_ref[...]
    next_ref[...] = update_items(
        exact, exact.astype(BF16), shrinkage * count.astype(F32), low_ref, rated_ref,
        residual_ref, item_ref,
    )


def item_body(slot, stops, parity, last, arrivals, *refs):
    sources = refs[:arrivals]
    held_ref, low_ref, rated_ref, decay_ref = refs[arrivals : arrivals + 4]
    others = refs[arrivals + 4 : -3]
    next_ref, residual_ref, item_ref = refs[-3:]
    active, _, crossed, own = plan_slot(slot, stops)

    def emit(block):
        if last:
            groups, halves, rows, columns = next_ref.shape
            for h in range(halves):
                half = block[:, h * columns : (h + 1) * columns]
                next_ref[:, h] = half.reshape(groups, rows, columns)
        else:
            next_ref[...] = block

    @pl.when(jnp.logical_and(own == parity, active))
    def _():
        item_low = sources[0][...]
        if arrivals == 2:
            item_low = jnp.where(crossed, sources[1][...], item_low)
        emit(
            update_items(
                item_low.astype(F32), item_low, decay_ref[0:1, :], low_ref, rated_ref,
                residual_ref, item_ref,
            )
        )

    @pl.when(jnp.logical_and(own == parity, jnp.logical_not(active)))
    def _():
        emit(held_ref[...])

    if others:

        @pl.when(own != parity)
        def _():
            emit(others[0][...])
            residual_ref[...] = others[1][...]
            item_ref[...] = others[2][...]


def user_body(slot, stops, last, count_ref, row_ref, residual_ref, item_ref, user_ref, *refs):
    active, stop, _, _ = plan_slot(slot, stops)
    count = jnp.where(active, count_ref[stop], 0)
    if last:
        (out_ref,) = refs
    else:
        ratings_ref, out_ref, low_ref, rated_ref, decay_ref = refs
        next_active, next_stop, _, _ = plan_slot(slot + 1, stops)
        next_count = jnp.where(next_active, count_ref[next_stop], 0)
        decay_ref[...] = jnp.full(decay_ref.shape, shrinkage * next_count.astype(F32))
    tile = item_ref.shape[0]
    if last or slot == 0:
        out_ref[...] = user_ref[...]
    for c in range(residual_ref.shape[1] // tile):

        @pl.when(c < count)
        def _():
            step = lax.dot_general(
                residual_ref[:, c * tile : (c + 1) * tile],
                item_ref[...],
                (((0,), (0,)), ((), ())),
                preferred_element_type=F32,
            )
            rows = pl.ds(pl.multiple_of(row_ref[c, stop] * tile, tile), tile)
            before = user_ref[rows, :]
            out_ref[rows, :] = before + learn_rate * (step - shrinkage * before)

    if not last:

        @pl.when(next_active)
        def _():
            fetch(next_stop, next_count, row_ref, out_ref, low_ref, rated_ref, ratings_ref)


def route_body(stops, plan_ref, index_ref, filled):
    groups, blocks = plan_ref.shape
    group = lax.rem(lax.axis_index("group") + groups - 1, groups)
    turned = lax.rem(group, GROUP_ROW) == GROUP_ROW - 1

    @pl.loop(0, blocks)
    def _(d):
        filled[d] = 0
        for c in range(CAP):
            index_ref[d * CAP + c] = blocks

    @pl.loop(0, blocks)
    def _(k):
        dest = plan_ref[group, k]
        place = filled[dest]
        filled[dest] = place + 1
        at = lax.rem(k + (stops - 1), blocks)
        inner = lax.rem(at, PLANE)
        index_ref[dest * CAP + place] = jnp.where(turned, blocks - PLANE - at + 2 * inner, at)


def pick_body(index_ref, pieces_ref, out_ref, held):
    blocks = pieces_ref.shape[0]
    held[pl.ds(0, blocks)] = pieces_ref[...]
    held[blocks] = jnp.zeros(held.shape[1:], held.dtype)

    @pl.loop(0, out_ref.shape[0], unroll=16)
    def _(d):
        for c in range(CAP):
            out_ref[d, c] = held[index_ref[d * CAP + c]]


def place_body(pieces_ref, out_ref):
    groups, halves, slots, rows, columns = pieces_ref.shape
    for c in range(slots):
        for h in range(halves):
            out_ref[c, :, h * columns : (h + 1) * columns] = pieces_ref[:, h, c].reshape(
                groups * rows, columns
            )


def shards(user_factors, item_factors, ratings, tile_rows, counts, plan):
    users = user_factors[0]
    rating_tiles = ratings[0, 0]
    row_table = tile_rows[0, 0].T
    count_table = counts[0, 0]
    stops, tiles_at_stop, tile, _ = rating_tiles.shape
    blocks = lax.axis_size("blk")
    groups = lax.axis_size("group")
    items, rank = item_factors.shape[1:]
    wide = tiles_at_stop * tile
    slots = stops + LAG

    low_shape = jax.ShapeDtypeStruct((wide, rank), BF16)
    rated_shape = jax.ShapeDtypeStruct((items, wide), BF16)
    block_shape = jax.ShapeDtypeStruct((items, rank), BF16)
    decay_shape = jax.ShapeDtypeStruct((8, rank), F32)
    piece_shape = jax.ShapeDtypeStruct((items // 8, rank // 128, 8, 128), BF16)
    user_shape = jax.ShapeDtypeStruct(users.shape, F32)
    tile_scratch = [pltpu.VMEM((tiles_at_stop, tile, tile), BF16), pltpu.SemaphoreType.DMA]
    block, residual, item_low = call(
        first_body,
        (block_shape, rated_shape, block_shape),
        [HBM] * 5,
        (VMEM, VMEM, VMEM),
        [
            pltpu.SMEM(count_table.shape, jnp.int32),
            pltpu.SMEM(row_table.shape, jnp.int32),
            pltpu.VMEM(users.shape, F32),
            pltpu.VMEM((items, rank), F32),
            tile_scratch[0],
            pltpu.VMEM(low_shape.shape, BF16),
            pltpu.VMEM(rated_shape.shape, BF16),
            pltpu.SemaphoreType.DMA((5,)),
        ],
        4 * items * wide * rank,
        limit=FIRST_LIMIT,
    )(count_table, row_table, users, item_factors[0], rating_tiles)

    across = [(b, (b + 1) % blocks) for b in range(PLANE - 1, blocks, PLANE)]

    def within(slot, parity):
        pairs = []
        for b in range(blocks):
            inner = b % PLANE
            if inner % 2 == parity and inner != PLANE - 1:
                here, there = stop_at(slot, inner, stops), stop_at(slot + 1, inner + 1, stops)
                if here is not None and there == here + 1:
                    pairs.append((b, b + 1))
        return pairs

    odd_block = block
    from_odd = from_even = None
    crossing = {}
    for slot in range(slots):
        last = slot == slots - 1

        def items_call(parity, arrived, others):
            ends = last and parity == 0
            return call(
                functools.partial(item_body, slot, stops, parity, ends, len(arrived)),
                (piece_shape if ends else block_shape, rated_shape, block_shape),
                [VMEM] * (len(arrived) + 4 + len(others)),
                (VMEM, VMEM, VMEM),
                (),
                2 * items * wide * rank,
            )(*arrived, block, low, rated, decay, *others)

        if slot > 0:
            others = items_call(1, [from_even], ())
            odd_block = others[0]
        arrived = [from_odd] + ([crossing[slot]] if slot in crossing else [])
        if not last:
            from_odd = lax.ppermute(odd_block, "blk", within(slot, 1))
        if slot < stops - 1:
            crossing[slot + 1 + LAG] = lax.ppermute(odd_block, "blk", across)
        if slot > 0:
            block, residual, item_low = items_call(0, arrived, others)
        if not last:
            from_even = lax.ppermute(block, "blk", within(slot, 0))
        body = functools.partial(user_body, slot, stops, last)
        operands = (count_table, row_table, residual, item_low, users)
        flops = 2 * wide * items * rank
        if last:
            users = call(
                body, user_shape, [SMEM, SMEM, VMEM, VMEM, VMEM], VMEM, (), flops
            )(*operands)
        else:
            users, low, rated, decay = call(
                body,
                (user_shape, low_shape, rated_shape, decay_shape),
                [SMEM, SMEM, VMEM, VMEM, VMEM, VMEM],
                (VMEM, VMEM, VMEM, VMEM),
                (),
                flops,
                alias={4: 0} if slot else {},
            )(*operands, rating_tiles)

    pieces = block.reshape(blocks, -1, 128)
    index = call(
        functools.partial(route_body, stops),
        jax.ShapeDtypeStruct((blocks * CAP,), jnp.int32),
        [SMEM],
        SMEM,
        [pltpu.SMEM((blocks,), jnp.int32)],
        moved=4 * blocks,
    )(plan)
    moves = []
    for b in range(blocks):
        for g in range(groups):
            to_b, to_g = hand_over(b, g, blocks, groups)
            moves.append((b * groups + g, to_b * groups + to_g))
    shifted = lax.ppermute(pieces, ("blk", "group"), moves)
    spread = lax.all_to_all(shifted, "blk", split_axis=0, concat_axis=0, tiled=True)
    picked = call(
        pick_body,
        jax.ShapeDtypeStruct((blocks, CAP) + pieces.shape[1:], BF16),
        [SMEM, VMEM],
        VMEM,
        [pltpu.VMEM((blocks + 1,) + pieces.shape[1:], BF16)],
    )(index, spread)
    landed = lax.all_to_all(picked, "blk", split_axis=0, concat_axis=0, tiled=True)
    landed = landed.reshape(blocks, CAP, -1, 8, 128).transpose(0, 2, 1, 3, 4)
    received = call(
        place_body, jax.ShapeDtypeStruct((CAP, items, rank), BF16), [VMEM], VMEM
    )(landed.reshape(items // 8, rank // 128, CAP, 8, 128))
    return (users[None], received[None, None])


def solution(mesh):
    in_specs = (
        P("group", "blk", None),
        P("group", "blk", None),
        P("group", "blk", None, None, None, None),
        P("group", "blk", None, None),
        P("group", "blk", None),
        P(),
    )
    out_specs = (P("group", "blk", None), P("group", "blk", None, None, None))
    return jax.shard_map(shards, mesh=mesh, in_specs=in_specs, out_specs=out_specs, check_vma=False)
```
